256 devices in a mesh: ctx: 128 (over x, y, z), head: 2 (over core).
Axes of the slice: x: 4, y: 4, z: 8, core: 2. Of those that a mesh axis runs over, the one named last changes fastest.
Arguments:
- queries: bfloat16 [16384, 3072], P('ctx', 'head'), may hold values from -6 to 6
- keys: bfloat16 [16384, 3072], P('ctx', 'head'), may hold values from -6 to 6
- values: bfloat16 [16384, 3072], P('ctx', 'head'), may hold values from -30 to 30
- decay_log: float32 [32, 16384], P('head', 'ctx'), may hold values from -1 to 0
- norm_gain: float32 [3072], P('head'), may hold values from 0.25 to 1.75
- out_grad: bfloat16 [16384, 3072], P('ctx', 'head'), may hold values from -6 to 6
- doc_lengths: int32 [16], replicated, may hold values from 1 to 4096, 16384 in all
Outputs:
- attn_output: bfloat16 [16384, 3072], P('ctx', 'head')
- query_grad: bfloat16 [16384, 3072], P('ctx', 'head')
- key_grad: bfloat16 [16384, 3072], P('ctx', 'head')
- value_grad: bfloat16 [16384, 3072], P('ctx', 'head')
The draws below stay inside these ranges and needn't reach their ends.
Inputs may be any that keep to these rules, and one draw needn't show every extreme that they name: `doc_lengths`: the 16 lengths sum to 16384; the longest is exactly 4096.
All inputs are finite; a program needn't handle non-finite values.
Results may differ from the reference program's by a relative error of at most 0.01.
Values sent between devices are 32-bit elements; how exact they have to be, the bound alone decides.
A program may use at most 256 MiB of HBM per device.

```python
import math
import jax
import jax.numpy as jnp
import numpy as np
from jax import lax

HEAD_TOTAL = 32
HEAD_DIM = 96
TOK_DEV = 128
NDOCS = 16
TOKEN_TOTAL = 16384
FEAT = 3072
MOST_DOC = 4096


def draw_values(key, part):
    head_key, noise_key = jax.random.split(jax.random.fold_in(key, 11))
    position = jnp.arange(HEAD_TOTAL, dtype=jnp.float32) / HEAD_TOTAL
    jitter = jax.random.uniform(head_key, (HEAD_TOTAL,), minval=0.8, maxval=1.25)
    ramp = jnp.exp(math.log(0.4) + position * math.log(10.0))
    base = jnp.clip(jax.random.normal(noise_key, (TOKEN_TOTAL, HEAD_TOTAL, HEAD_DIM)), -6.0, 6.0)
    scaled = base * (ramp * jitter)[None, :, None]
    return scaled.reshape(TOKEN_TOTAL, HEAD_TOTAL * HEAD_DIM).astype(jnp.bfloat16)


def draw_decay_log(key, part):
    segment_keys = jax.random.split(jax.random.fold_in(key, 23), 7)
    fast_share = 0.5
    fast = jax.random.uniform(segment_keys[0], (HEAD_TOTAL,)) < fast_share
    fast_rate = jnp.exp(jax.random.uniform(segment_keys[1], (HEAD_TOTAL,), minval=math.log(1.0 / 50.0), maxval=math.log(1.0 / 30.0)))
    slow_rate = math.log(10.0) / TOKEN_TOTAL * jax.random.uniform(segment_keys[2], (HEAD_TOTAL,), minval=0.05, maxval=0.4)
    base_rate = jnp.where(fast, fast_rate, slow_rate)
    blocks = TOKEN_TOTAL // TOK_DEV
    block_factor = jnp.exp(jax.random.uniform(segment_keys[3], (HEAD_TOTAL, blocks), minval=math.log(0.5), maxval=math.log(2.0)))
    rough = jax.random.uniform(segment_keys[4], (HEAD_TOTAL, TOKEN_TOTAL), minval=0.5, maxval=1.5)
    token_wise = base_rate[:, None] * jnp.repeat(block_factor, TOK_DEV, axis=1) * rough
    sudden_spike = jax.random.uniform(segment_keys[5], (TOKEN_TOTAL,)) < 4.0 / TOKEN_TOTAL
    spike_penalty = jax.random.uniform(segment_keys[6], (HEAD_TOTAL, TOKEN_TOTAL), minval=0.2, maxval=0.5)
    spike_logits = jnp.where(sudden_spike[None, :], jnp.log(1.0 - spike_penalty), 0.0)
    return (spike_logits - token_wise).astype(jnp.float32)


def block_scale(stream_key, extent, cuts, smallest, high):
    factor_of, own = 1.0, jax.random.fold_in(stream_key, 6)
    for dim, blocks in cuts:
        heights = jnp.exp(jax.random.uniform(jax.random.fold_in(own, dim), (blocks,), jnp.float32, smallest / len(cuts), high / len(cuts)))
        factor_of = factor_of * jnp.repeat(heights, extent[dim] // blocks).reshape([-1 if axis == dim else 1 for axis in range(len(extent))])
    return factor_of


def length_profile(number_of, total, reach, skew):
    weights = [(1 << 20) // math.isqrt(grade ** skew) + 1 for grade in range(2, number_of + 1)]
    surplus, holding = total - reach - (number_of - 1), [1] * (number_of - 1)
    while surplus > 0:
        free = [i for i in range(number_of - 1) if holding[i] < reach]
        whole, remaining = sum([weights[i] for i in free]), surplus
        for i in free:
            more = min(reach - holding[i], max(1, remaining * weights[i] // whole), surplus)
            holding[i] = holding[i] + more
            surplus = surplus - more
    return np.array([reach] + holding)


def ragged_sizes(stream_key, count, total, reach, skew):
    if count == 2:
        one = jax.random.randint(stream_key, (), max(1, total - reach), min(reach, total - 1) + 1)
        return jnp.stack([one, total - one])
    lengths = jnp.asarray(length_profile(count, total, reach, skew), jnp.int32)
    pairs = (count - 1) // 2
    giver, receiver = lengths[1:1 + 2 * pairs:2], lengths[2:2 + 2 * pairs:2]
    room = jnp.minimum(giver - 1, reach - receiver)
    passed = jax.random.randint(jax.random.fold_in(stream_key, 1), (pairs,), 0, 1 << 20) % (room + 1)
    lengths = lengths.at[1:1 + 2 * pairs:2].set(giver - passed).at[2:2 + 2 * pairs:2].set(receiver + passed)
    return lengths[jax.random.permutation(jax.random.fold_in(stream_key, 2), count)]


def gaussian(own_key, extent, spread, reach, shards=(), held_as=jnp.bfloat16):
    result = spread * jax.random.normal(own_key, extent, jnp.float32)
    if shards:
        result = result * block_scale(own_key, extent, shards, -0.22, 0.18)
    return jnp.clip(result, -reach, reach).astype(held_as)


def setup_inputs(seed: int = 0) -> dict:
    seeds = jax.random.split(jax.random.key(seed), 8)
    queries = gaussian(seeds[0], (TOKEN_TOTAL, FEAT), 1.0, 6.0, ((0, 128), (1, 2)))
    keys = gaussian(seeds[1], (TOKEN_TOTAL, FEAT), 1.0, 6.0, ((0, 128), (1, 2)))
    values = draw_values(jax.random.fold_in(seeds[7], 71), 0)
    decay_log = draw_decay_log(jax.random.fold_in(seeds[7], 71), 0)
    norm_gain = jnp.clip(1.0 + 0.15 * jax.random.normal(seeds[4], (FEAT,), jnp.float32), 0.25, 1.75)
    out_grad = gaussian(seeds[5], (TOKEN_TOTAL, FEAT), 1.0, 6.0, ((0, 128), (1, 2)))
    doc_lengths = ragged_sizes(seeds[6], NDOCS, TOKEN_TOTAL, MOST_DOC, 2).astype(jnp.int32)
    return dict(queries=queries, keys=keys, values=values, decay_log=decay_log, norm_gain=norm_gain, out_grad=out_grad, doc_lengths=doc_lengths)


HIGHEST = lax.Precision.HIGHEST
EPSILON = 1e-06

def doc_starts(doc_lengths):
    doc_ends = jnp.cumsum(doc_lengths).astype(jnp.int32)
    return (doc_ends - doc_lengths).astype(jnp.int32)

def geometry(decay_block, block_start, starts_doc):
    row_count = decay_block.shape[1]
    positions = (block_start + jnp.arange(row_count, dtype=jnp.int32)).astype(jnp.int32)
    doc_index = lax.optimization_barrier(jnp.sum((starts_doc[None, :] <= positions[:, None]).astype(jnp.int32), axis=1))
    doc_before = jnp.sum((starts_doc <= block_start - 1).astype(jnp.int32))
    carry_mask = (doc_index == doc_before).astype(decay_block.dtype)
    log_cum = jnp.cumsum(decay_block, axis=1)
    causal = positions[:, None] >= positions[None, :]
    same_doc = jnp.logical_and(causal, doc_index[:, None] == doc_index[None, :])
    log_gap = jnp.where(same_doc[None], log_cum[:, :, None] - log_cum[:, None, :], 0.0)
    decay_mask = jnp.exp(log_gap) * same_doc[None].astype(decay_block.dtype)
    keep_last = (doc_index == doc_index[row_count - 1]).astype(decay_block.dtype)
    exit_weight = jnp.exp(log_cum[:, row_count - 1:row_count] - log_cum) * keep_last[None, :]
    reach_in = carry_mask[None, :] * jnp.exp(log_cum)
    factor = reach_in[:, row_count - 1]
    return (decay_mask, exit_weight, reach_in, factor)

def rounded(array):
    return lax.optimization_barrier(array.astype(jnp.bfloat16)).astype(jnp.float32)

def reference(queries, keys, values, decay_log, norm_gain, out_grad, doc_lengths):
    head_count, seq_total = decay_log.shape
    feature_count = queries.shape[1]
    head_width = feature_count // head_count
    blocks = seq_total // TOK_DEV
    score_scale = 1.0 / math.sqrt(head_width)
    starts_doc = doc_starts(doc_lengths)

    def split(array):
        return array.reshape(blocks, TOK_DEV, head_count, head_width)
    query_blocks = split(queries)
    key_blocks = split(keys)
    value_blocks = split(values)
    grad_blocks = split(out_grad)
    decay_blocks = decay_log.reshape(head_count, blocks, TOK_DEV).transpose(1, 0, 2)
    block_starts = (jnp.arange(blocks, dtype=jnp.int32) * TOK_DEV).astype(jnp.int32)

    def exit_part(inputs):
        key_block, value_block, decay_block, block_start = inputs
        decay_mask, exit_weight, reach_in, factor = geometry(decay_block, block_start, starts_doc)
        key_f = key_block.astype(jnp.float32)
        value_f = value_block.astype(jnp.float32)
        block_state = jnp.einsum('shd,she->hde', key_f * exit_weight.T[:, :, None], value_f, precision=HIGHEST)
        return (factor, block_state)
    factors, states = lax.map(exit_part, (key_blocks, value_blocks, decay_blocks, block_starts))
    zero_state = jnp.zeros((head_count, head_width, head_width), jnp.float32)

    def chain_step(held, inputs):
        factor, block_state = inputs
        return (factor[:, None, None] * held + block_state, held)
    final_state, incoming = lax.scan(chain_step, zero_state, (factors, states))

    def middle(inputs):
        query_block, key_block, value_block, grad_block, decay_block, block_start, incoming_block = inputs
        decay_mask, exit_weight, reach_in, factor = geometry(decay_block, block_start, starts_doc)
        query_f = query_block.astype(jnp.float32)
        key_f = key_block.astype(jnp.float32)
        value_f = value_block.astype(jnp.float32)
        scores = jnp.einsum('thd,shd->hts', query_f, key_f, precision=HIGHEST)
        attn_probs = rounded(scores * score_scale * decay_mask)
        local_part = jnp.einsum('hts,shd->thd', attn_probs, value_f, precision=HIGHEST)
        carried = jnp.einsum('thd,hde->the', query_f, incoming_block, precision=HIGHEST)
        attended = (local_part + score_scale * reach_in.T[:, :, None] * carried).reshape(TOK_DEV, feature_count)
        inv_rms = lax.rsqrt(lax.optimization_barrier(jnp.sum(attended * attended, axis=1)) / feature_count + EPSILON)
        output_block = (attended * inv_rms[:, None] * norm_gain[None, :]).astype(jnp.bfloat16)
        grad_gain = grad_block.reshape(TOK_DEV, feature_count).astype(jnp.float32) * norm_gain[None, :]
        grad_dot = lax.optimization_barrier(jnp.sum(grad_gain * attended, axis=1))
        attended_grad = (grad_gain * inv_rms[:, None] - attended * (inv_rms ** 3 * grad_dot / feature_count)[:, None]).astype(jnp.bfloat16)
        grad_f = attended_grad.reshape(TOK_DEV, head_count, head_width).astype(jnp.float32)
        block_grad = score_scale * jnp.einsum('thd,the->hde', query_f * reach_in.T[:, :, None], grad_f, precision=HIGHEST)
        return (output_block, attended_grad, block_grad)
    outputs, attended_grads, block_grads = lax.map(middle, (query_blocks, key_blocks, value_blocks, grad_blocks, decay_blocks, block_starts, incoming))
    final_grad, later = lax.scan(chain_step, zero_state, (factors, block_grads), reverse=True)

    def finish(inputs):
        query_block, key_block, value_block, attended_grad, decay_block, block_start, incoming_block, later_block = inputs
        decay_mask, exit_weight, reach_in, factor = geometry(decay_block, block_start, starts_doc)
        query_f = query_block.astype(jnp.float32)
        key_f = key_block.astype(jnp.float32)
        value_f = value_block.astype(jnp.float32)
        grad_f = attended_grad.reshape(TOK_DEV, head_count, head_width).astype(jnp.float32)
        scores = jnp.einsum('thd,shd->hts', query_f, key_f, precision=HIGHEST)
        attn_probs = rounded(scores * score_scale * decay_mask)
        grad_scores = jnp.einsum('thd,shd->hts', grad_f, value_f, precision=HIGHEST)
        score_grad = rounded(grad_scores * score_scale * decay_mask)
        query_part = jnp.einsum('hts,shd->thd', score_grad, key_f, precision=HIGHEST)
        query_part = query_part + score_scale * reach_in.T[:, :, None] * jnp.einsum('the,hde->thd', grad_f, incoming_block, precision=HIGHEST)
        key_part = jnp.einsum('hts,thd->shd', score_grad, query_f, precision=HIGHEST)
        key_part = key_part + exit_weight.T[:, :, None] * jnp.einsum('she,hde->shd', value_f, later_block, precision=HIGHEST)
        value_part = jnp.einsum('hts,the->she', attn_probs, grad_f, precision=HIGHEST)
        value_part = value_part + exit_weight.T[:, :, None] * jnp.einsum('shd,hde->she', key_f, later_block, precision=HIGHEST)
        return (query_part.reshape(TOK_DEV, feature_count).astype(jnp.bfloat16), key_part.reshape(TOK_DEV, feature_count).astype(jnp.bfloat16), value_part.reshape(TOK_DEV, feature_count).astype(jnp.bfloat16))
    query_grads, key_grads, value_grads = lax.map(finish, (query_blocks, key_blocks, value_blocks, attended_grads, decay_blocks, block_starts, incoming, later))
    return (outputs.reshape(seq_total, feature_count), query_grads.reshape(seq_total, feature_count), key_grads.reshape(seq_total, feature_count), value_grads.reshape(seq_total, feature_count))
```

```python
import functools
import math

import jax
import jax.numpy as jnp
from jax import lax
from jax.experimental import pallas as pl
from jax.experimental.pallas import tpu as pltpu
from jax.sharding import PartitionSpec as P

EPSILON = 1e-06
MESH = pl.DeviceIdType.MESH
F32 = jnp.float32
BF16 = jnp.bfloat16

RING = 8
REACH = 4
GROUP = 4
OFFSETS = (1, -1, 2, -2, 3, -3, 4)
PIECES = 2


def contract(a, b, ca, cb):
    return lax.dot_general(a, b, (((ca,), (cb,)), ((), ())), preferred_element_type=F32)


def split_pair(x):
    high = x.astype(BF16)
    return high, (x - high.astype(F32)).astype(BF16)


def kernel(
    head_dim,
    feature_count,
    lines,
    docs,
    q_ref,
    k_ref,
    v_ref,
    decay_ref,
    gain_ref,
    og_ref,
    o_ref,
    dq_ref,
    dk_ref,
    dv_ref,
    att,
    grad,
    crx,
    xw,
    cm,
    probs,
    kpart,
    vpart,
    send_a,
    recv_a,
    back_a,
    come_a,
    send_b,
    recv_b,
    back_b,
    come_b,
    tot_a,
    rtot_a,
    tot_b,
    rtot_b,
    fac,
    rfac,
    lfac,
    rlfac_a,
    rlfac_b,
    sums,
    rsums,
    there_s,
    there_r,
    line_s,
    line_r,
    back_s,
    back_r,
    fac_s,
    fac_r,
    lfac_s,
    lfac_r,
    sum_s,
    sum_r,
):
    rows = q_ref.shape[0]
    width = GROUP * head_dim
    groups = q_ref.shape[1] // width
    half = head_dim // 2
    scale = 1.0 / math.sqrt(head_dim)
    place = lax.axis_index("ctx")
    core = lax.axis_index("head")
    z = lax.rem(place, RING)
    line = lax.div(place, RING)

    def in_line(other):
        return (line * RING + other, core)

    def ring(offset):
        return lax.rem(z + (offset + RING), RING)

    def other_line(offset):
        return (lax.rem(line + (offset + lines), lines) * RING + z, core)

    barrier = pltpu.get_barrier_semaphore()
    partners = [in_line(ring(k)) for k in OFFSETS]
    partners += [other_line(s * k) for k in range(1, REACH + 1) for s in (1, -1)]
    partners += [(place, 1 - core)]
    for device in partners:
        pl.semaphore_signal(barrier, inc=1, device_id=device, device_id_type=MESH)

    start = place * rows
    col = start + lax.broadcasted_iota(jnp.int32, (rows, 1), 0)
    row = start + lax.broadcasted_iota(jnp.int32, (1, rows), 1)
    doc_col = jnp.zeros((rows, 1), jnp.int32)
    doc_row = jnp.zeros((1, rows), jnp.int32)
    before = jnp.int32(0)
    last = jnp.int32(0)
    begins = jnp.int32(0)
    for i in range(docs.shape[0]):
        doc_col += (begins <= col).astype(jnp.int32)
        doc_row += (begins <= row).astype(jnp.int32)
        before += (begins <= start - 1).astype(jnp.int32)
        last += (begins <= start + (rows - 1)).astype(jnp.int32)
        begins = begins + docs[i]
    carried_in = (doc_col == before).astype(F32)
    keep_last = (doc_col == last).astype(F32)
    same = jnp.logical_and(col >= row, doc_col == doc_row)

    decay = decay_ref[...]
    ti = lax.broadcasted_iota(jnp.int32, (rows, rows), 0)
    si = lax.broadcasted_iota(jnp.int32, (rows, rows), 1)
    lower = (si <= ti).astype(F32)
    log_col = lax.dot_general(
        lower, decay, (((1,), (1,)), ((), ())),
        precision=lax.Precision.HIGHEST, preferred_element_type=F32,
    )
    log_row = lax.dot_general(
        decay, lower, (((1,), (1,)), ((), ())),
        precision=lax.Precision.HIGHEST, preferred_element_type=F32,
    )
    exit_col = jnp.exp(log_col[rows - 1 : rows, :] - log_col) * keep_last
    reach_col = carried_in * jnp.exp(log_col)

    lane = lax.broadcasted_iota(jnp.int32, (1, width), 1)
    is_head = [
        jnp.logical_and(lane >= i * head_dim, lane < (i + 1) * head_dim) for i in range(GROUP)
    ]
    head_one = [m.astype(F32).astype(BF16) for m in is_head]

    def spread(columns, g):
        out = columns[:, g * GROUP + GROUP - 1 : g * GROUP + GROUP]
        for i in reversed(range(GROUP - 1)):
            out = jnp.where(is_head[i], columns[:, g * GROUP + i : g * GROUP + i + 1], out)
        return out

    def lanes(g):
        return slice(g * width, (g + 1) * width)

    def pick(square):
        out = square[(GROUP - 1) * head_dim :, :]
        for i in reversed(range(GROUP - 1)):
            out = jnp.where(is_head[i], square[i * head_dim : (i + 1) * head_dim, :], out)
        return out

    def stack(x):
        return jnp.concatenate([x * m for m in head_one], axis=0)

    def put_state(buf, g, state):
        buf[2 * g] = state[:half, :]
        buf[2 * g + 1] = state[half:, :]

    def block_diagonal(buf, g):
        state = jnp.concatenate([buf[2 * g], buf[2 * g + 1]], axis=0)
        high, low = split_pair(state)
        return stack(high), stack(low)

    for g in range(groups):
        ex = spread(exit_col, g)
        xw[:, lanes(g)] = ex
        rx = spread(reach_col, g)
        crx[:, lanes(g)] = rx * scale
        fac[2 * g] = rx[rows - 1 : rows, :]
        fac[2 * g + 1] = rx[rows - 1 : rows, :]
        high, low = split_pair(k_ref[:, lanes(g)].astype(F32) * ex)
        v = v_ref[:, lanes(g)]
        put_state(send_a, g, pick(contract(high, v, 0, 0) + contract(low, v, 0, 0)))

    pl.semaphore_wait(barrier, len(partners))

    step = half // PIECES

    def there(phase, src, dst):
        copies = []
        for j in range(PIECES):
            part = pl.ds(j * step, step)
            these = []
            for i, k in enumerate(OFFSETS):
                other = ring(k)
                copy = pltpu.make_async_remote_copy(
                    src_ref=src.at[other, part],
                    dst_ref=dst.at[z, part],
                    send_sem=there_s.at[phase, j, i],
                    recv_sem=there_r.at[phase, j, i],
                    device_id=in_line(other),
                    device_id_type=MESH,
                )
                copy.start()
                these.append(copy)
            copies.append(these)
        return copies

    fac_copies = []
    for i, k in enumerate(OFFSETS):
        other = ring(k)
        copy = pltpu.make_async_remote_copy(
            src_ref=fac.at[other],
            dst_ref=rfac.at[z],
            send_sem=fac_s.at[i],
            recv_sem=fac_r.at[i],
            device_id=in_line(other),
            device_id_type=MESH,
        )
        copy.start()
        fac_copies.append(copy)
    there_a = there(0, send_a, recv_a)
    rfac[z] = fac[z]
    recv_a[z] = send_a[z]

    for g in range(groups):
        for i in range(GROUP):
            h = g * GROUP + i
            gap = log_col[:, h : h + 1] - log_row[h : h + 1, :]
            cm[g, :, i * rows : (i + 1) * rows] = scale * jnp.exp(jnp.where(same, gap, -1e30))
        scores = contract(q_ref[:, lanes(g)], stack(k_ref[:, lanes(g)]), 1, 1)
        p = (scores * cm[g]).astype(BF16)
        probs[g] = p
        att[:, lanes(g)] = contract(p, stack(v_ref[:, lanes(g)]), 1, 0)

    def owner(phase, sign, there_copies, src, total, rtotal, rlfac, dst, come):
        order = list(range(RING)) if sign > 0 else list(reversed(range(RING)))
        line_copies = []
        for j in range(PIECES):
            part = slice(j * step, (j + 1) * step)
            for copy in there_copies[j]:
                copy.wait()
            if j == 0:
                if phase == 0:
                    for copy in fac_copies:
                        copy.wait()
                    product = rfac[0]
                    for i in range(1, RING):
                        product = product * rfac[i]
                    lfac[0] = product
            run = src[order[0], part, :]
            for i in order[1:]:
                run = src[i, part, :] + rfac[i] * run
            total[part, :] = run
            these = []
            for k in range(1, REACH + 1):
                if j == 0:
                    copy = pltpu.make_async_remote_copy(
                        src_ref=lfac.at[0],
                        dst_ref=rlfac.at[k - 1],
                        send_sem=lfac_s.at[phase, k - 1],
                        recv_sem=lfac_r.at[phase, k - 1],
                        device_id=other_line(sign * k),
                        device_id_type=MESH,
                    )
                    copy.start()
                    these.append(copy)
                copy = pltpu.make_async_remote_copy(
                    src_ref=total.at[pl.ds(j * step, step)],
                    dst_ref=rtotal.at[k - 1, pl.ds(j * step, step)],
                    send_sem=line_s.at[phase, j, k - 1],
                    recv_sem=line_r.at[phase, j, k - 1],
                    device_id=other_line(sign * k),
                    device_id_type=MESH,
                )
                copy.start()
                these.append(copy)
            line_copies.append(these)
        back_copies = []
        for j in range(PIECES):
            part = slice(j * step, (j + 1) * step)
            for copy in line_copies[j]:
                copy.wait()
            run = rtotal[REACH - 1, part, :]
            for k in reversed(range(REACH - 1)):
                run = rtotal[k, part, :] + rlfac[k] * run
            for i in order:
                dst[i, part, :] = run
                run = src[i, part, :] + rfac[i] * run
            for i, k in enumerate(OFFSETS):
                other = ring(k)
                copy = pltpu.make_async_remote_copy(
                    src_ref=dst.at[other, pl.ds(j * step, step)],
                    dst_ref=come.at[z, pl.ds(j * step, step)],
                    send_sem=back_s.at[phase, j, i],
                    recv_sem=back_r.at[phase, j, i],
                    device_id=in_line(other),
                    device_id_type=MESH,
                )
                copy.start()
                back_copies.append(copy)
        come[z] = dst[z]
        return back_copies

    for copy in owner(0, 1, there_a, recv_a, tot_a, rtot_a, rlfac_a, back_a, come_a):
        copy.wait()

    square = jnp.zeros((rows, width), F32)
    inner = jnp.zeros((rows, width), F32)
    for g in range(groups):
        high, low = block_diagonal(come_a, g)
        q = q_ref[:, lanes(g)]
        full = att[:, lanes(g)] + crx[:, lanes(g)] * (
            contract(q, high, 1, 0) + contract(q, low, 1, 0)
        )
        att[:, lanes(g)] = full
        square += full * full
        inner += og_ref[:, lanes(g)].astype(F32) * gain_ref[:, lanes(g)] * full
    square = jnp.sum(square, axis=1, keepdims=True)
    inner = jnp.sum(inner, axis=1, keepdims=True)
    first = lax.broadcasted_iota(jnp.int32, (1, 128), 1) < 64
    sums[...] = jnp.where(first, square, inner)
    copy = pltpu.make_async_remote_copy(
        src_ref=sums,
        dst_ref=rsums,
        send_sem=sum_s,
        recv_sem=sum_r,
        device_id=(place, 1 - core),
        device_id_type=MESH,
    )
    copy.start()
    copy.wait()
    both = sums[...] + rsums[...]
    inv_rms = lax.rsqrt(both[:, 0:1] / feature_count + EPSILON)
    along = inv_rms * inv_rms * inv_rms * both[:, 64:65] / feature_count

    for g in range(groups):
        a = att[:, lanes(g)]
        gg = og_ref[:, lanes(g)].astype(F32) * gain_ref[:, lanes(g)]
        gr = (gg * inv_rms - a * along).astype(BF16)
        grad[:, lanes(g)] = gr
        high, low = split_pair(q_ref[:, lanes(g)].astype(F32) * crx[:, lanes(g)])
        put_state(send_b, g, pick(contract(high, gr, 0, 0) + contract(low, gr, 0, 0)))
    there_b = there(1, send_b, recv_b)
    recv_b[z] = send_b[z]

    for g in range(groups):
        gr = grad[:, lanes(g)]
        o_ref[:, lanes(g)] = (att[:, lanes(g)] * inv_rms * gain_ref[:, lanes(g)]).astype(BF16)
        grad_scores = contract(gr, stack(v_ref[:, lanes(g)]), 1, 1)
        sg = (grad_scores * cm[g]).astype(BF16)
        high, low = block_diagonal(come_a, g)
        dq = contract(sg, stack(k_ref[:, lanes(g)]), 1, 0) + crx[:, lanes(g)] * (
            contract(gr, high, 1, 1) + contract(gr, low, 1, 1)
        )
        dq_ref[:, lanes(g)] = dq.astype(BF16)
        p = probs[g]
        tall_p = jnp.concatenate([p[:, i * rows : (i + 1) * rows] for i in range(GROUP)], axis=0)
        tall_s = jnp.concatenate([sg[:, i * rows : (i + 1) * rows] for i in range(GROUP)], axis=0)
        kpart[:, lanes(g)] = contract(tall_s, stack(q_ref[:, lanes(g)]), 0, 0)
        vpart[:, lanes(g)] = contract(tall_p, stack(gr), 0, 0)

    for copy in owner(1, -1, there_b, recv_b, tot_b, rtot_b, rlfac_b, back_b, come_b):
        copy.wait()

    for g in range(groups):
        high, low = block_diagonal(come_b, g)
        v = v_ref[:, lanes(g)]
        k = k_ref[:, lanes(g)]
        ex = xw[:, lanes(g)]
        dk_ref[:, lanes(g)] = (
            kpart[:, lanes(g)] + ex * (contract(v, high, 1, 1) + contract(v, low, 1, 1))
        ).astype(BF16)
        dv_ref[:, lanes(g)] = (
            vpart[:, lanes(g)] + ex * (contract(k, high, 1, 0) + contract(k, low, 1, 0))
        ).astype(BF16)


def solution(mesh):
    lines = mesh.shape["ctx"] // RING
    cores = mesh.shape["head"]

    def on_device(queries, keys, values, decay_log, norm_gain, out_grad, doc_lengths):
        rows, local = queries.shape
        head_dim = local // decay_log.shape[0]
        width = GROUP * head_dim
        groups = local // width
        half = head_dim // 2
        assert groups * 2 == RING and half % (8 * PIECES) == 0
        vmem = pl.BlockSpec(memory_space=pltpu.VMEM)
        state = pltpu.VMEM((RING, half, width), F32)
        total = pltpu.VMEM((half, width), F32)
        totals = pltpu.VMEM((REACH, half, width), F32)
        wide = pltpu.VMEM((rows, local), F32)
        dma = pltpu.SemaphoreType.DMA
        n = len(OFFSETS)
        out = jax.ShapeDtypeStruct((rows, local), BF16)
        return pl.pallas_call(
            functools.partial(kernel, head_dim, local * cores, lines),
            out_shape=(out, out, out, out),
            in_specs=[pl.BlockSpec(memory_space=pltpu.SMEM)] + [vmem] * 6,
            out_specs=(vmem,) * 4,
            scratch_shapes=[
                wide,
                pltpu.VMEM((rows, local), BF16),
                wide,
                wide,
                pltpu.VMEM((groups, rows, GROUP * rows), F32),
                pltpu.VMEM((groups, rows, GROUP * rows), BF16),
                wide,
                wide,
                state, state, state, state,
                state, state, state, state,
                total, totals, total, totals,
                pltpu.VMEM((RING, 1, width), F32),
                pltpu.VMEM((RING, 1, width), F32),
                pltpu.VMEM((1, 1, width), F32),
                pltpu.VMEM((REACH, 1, width), F32),
                pltpu.VMEM((REACH, 1, width), F32),
                pltpu.VMEM((rows, 128), F32),
                pltpu.VMEM((rows, 128), F32),
                dma((2, PIECES, n)), dma((2, PIECES, n)),
                dma((2, PIECES, REACH)), dma((2, PIECES, REACH)),
                dma((2, PIECES, n)), dma((2, PIECES, n)),
                dma((n,)), dma((n,)),
                dma((2, REACH)), dma((2, REACH)),
                dma, dma,
            ],
            compiler_params=pltpu.CompilerParams(collective_id=0, has_side_effects=True),
        )(
            doc_lengths,
            queries,
            keys,
            values,
            decay_log,
            norm_gain.reshape(1, local),
            out_grad,
        )

    return jax.shard_map(
        on_device,
        mesh=mesh,
        in_specs=(
            P("ctx", "head"),
            P("ctx", "head"),
            P("ctx", "head"),
            P("head", "ctx"),
            P("head"),
            P("ctx", "head"),
            P(),
        ),
        out_specs=(P("ctx", "head"),) * 4,
        check_vma=False,
    )
```

```python
import functools
import math

import jax
import jax.numpy as jnp
from jax import lax
from jax.experimental import pallas as pl
from jax.experimental.pallas import tpu as pltpu
from jax.sharding import PartitionSpec as P

EPSILON = 1e-06
MESH = pl.DeviceIdType.MESH
F32 = jnp.float32
BF16 = jnp.bfloat16

RING = 8
REACH = 4
GROUP = 4
OFFSETS = (1, -1, 2, -2, 3, -3, 4)
PIECES = 3
LAG = 1


def contract(a, b, ca, cb):
    return lax.dot_general(a, b, (((ca,), (cb,)), ((), ())), preferred_element_type=F32)


def kernel(
    head_dim,
    feature_count,
    lines,
    docs,
    q_ref,
    k_ref,
    v_ref,
    decay_ref,
    gain_ref,
    og_ref,
    o_ref,
    dq_ref,
    dk_ref,
    dv_ref,
    att,
    grad,
    crx,
    xw,
    cm,
    probs,
    kpart,
    vpart,
    send_a,
    recv_a,
    back_a,
    come_a,
    send_b,
    recv_b,
    back_b,
    come_b,
    tot_a,
    rtot_a,
    tot_b,
    rtot_b,
    fac,
    rfac,
    lfac,
    rlfac_a,
    rlfac_b,
    sums,
    rsums,
    there_s,
    there_r,
    line_s,
    line_r,
    back_s,
    back_r,
    fac_s,
    fac_r,
    lfac_s,
    lfac_r,
    sum_s,
    sum_r,
):
    rows = q_ref.shape[0]
    width = GROUP * head_dim
    groups = q_ref.shape[1] // width
    half = head_dim // 2
    scale = 1.0 / math.sqrt(head_dim)
    place = lax.axis_index("ctx")
    core = lax.axis_index("head")
    z = lax.rem(place, RING)
    line = lax.div(place, RING)

    def in_line(other):
        return (line * RING + other, core)

    def ring(offset):
        return lax.rem(z + (offset + RING), RING)

    def other_line(offset):
        return (lax.rem(line + (offset + lines), lines) * RING + z, core)

    barrier = pltpu.get_barrier_semaphore()
    partners = [in_line(ring(k)) for k in OFFSETS]
    partners += [other_line(s * k) for k in range(1, REACH + 1) for s in (1, -1)]
    partners += [(place, 1 - core)]
    for device in partners:
        pl.semaphore_signal(barrier, inc=1, device_id=device, device_id_type=MESH)

    start = place * rows
    col = start + lax.broadcasted_iota(jnp.int32, (rows, 1), 0)
    row = start + lax.broadcasted_iota(jnp.int32, (1, rows), 1)
    doc_col = jnp.zeros((rows, 1), jnp.int32)
    doc_row = jnp.zeros((1, rows), jnp.int32)
    before = jnp.int32(0)
    last = jnp.int32(0)
    begins = jnp.int32(0)
    for i in range(docs.shape[0]):
        doc_col += (begins <= col).astype(jnp.int32)
        doc_row += (begins <= row).astype(jnp.int32)
        before += (begins <= start - 1).astype(jnp.int32)
        last += (begins <= start + (rows - 1)).astype(jnp.int32)
        begins = begins + docs[i]
    carried_in = (doc_col == before).astype(F32)
    keep_last = (doc_col == last).astype(F32)
    same = jnp.logical_and(col >= row, doc_col == doc_row)

    decay = decay_ref[...]
    ti = lax.broadcasted_iota(jnp.int32, (rows, rows), 0)
    si = lax.broadcasted_iota(jnp.int32, (rows, rows), 1)
    lower = (si <= ti).astype(F32)
    log_col = lax.dot_general(
        lower, decay, (((1,), (1,)), ((), ())),
        precision=lax.Precision.HIGHEST, preferred_element_type=F32,
    )
    log_row = lax.dot_general(
        decay, lower, (((1,), (1,)), ((), ())),
        precision=lax.Precision.HIGHEST, preferred_element_type=F32,
    )
    exit_col = jnp.exp(log_col[rows - 1 : rows, :] - log_col) * keep_last
    reach_col = carried_in * jnp.exp(log_col)

    lane = lax.broadcasted_iota(jnp.int32, (1, width), 1)
    is_head = [
        jnp.logical_and(lane >= i * head_dim, lane < (i + 1) * head_dim) for i in range(GROUP)
    ]
    head_one = [m.astype(F32).astype(BF16) for m in is_head]

    def spread(columns, g):
        out = columns[:, g * GROUP + GROUP - 1 : g * GROUP + GROUP]
        for i in reversed(range(GROUP - 1)):
            out = jnp.where(is_head[i], columns[:, g * GROUP + i : g * GROUP + i + 1], out)
        return out

    def lanes(g):
        return slice(g * width, (g + 1) * width)

    def gain(g):
        tiles = width // 128
        return jnp.concatenate(
            [gain_ref[i : i + 1, :] for i in range(g * tiles, (g + 1) * tiles)], axis=1
        )

    def pick(square):
        out = square[(GROUP - 1) * head_dim :, :]
        for i in reversed(range(GROUP - 1)):
            out = jnp.where(is_head[i], square[i * head_dim : (i + 1) * head_dim, :], out)
        return out

    def stack(x):
        return jnp.concatenate([x * m for m in head_one], axis=0)

    def put_state(buf, g, state):
        buf[2 * g] = state[:half, :]
        buf[2 * g + 1] = state[half:, :]

    def block_diagonal(buf, g):
        state = jnp.concatenate([buf[2 * g], buf[2 * g + 1]], axis=0)
        return stack(state.astype(BF16))

    for g in range(groups):
        ex = spread(exit_col, g)
        xw[:, lanes(g)] = ex
        rx = spread(reach_col, g)
        crx[:, lanes(g)] = rx * scale
        fac[2 * g] = rx[rows - 1 : rows, :]
        fac[2 * g + 1] = rx[rows - 1 : rows, :]
        weighted = (k_ref[:, lanes(g)].astype(F32) * ex).astype(BF16)
        put_state(send_a, g, pick(contract(weighted, v_ref[:, lanes(g)], 0, 0)))

    pl.semaphore_wait(barrier, len(partners))

    step = half // PIECES

    def there(phase, src, dst):
        copies = []
        for j in range(PIECES):
            part = pl.ds(j * step, step)
            these = []
            for i, k in enumerate(OFFSETS):
                other = ring(k)
                copy = pltpu.make_async_remote_copy(
                    src_ref=src.at[other, part],
                    dst_ref=dst.at[z, part],
                    send_sem=there_s.at[phase, j, i],
                    recv_sem=there_r.at[phase, j, i],
                    device_id=in_line(other),
                    device_id_type=MESH,
                )
                copy.start()
                these.append(copy)
            copies.append(these)
        return copies

    fac_copies = []
    for i, k in enumerate(OFFSETS):
        other = ring(k)
        copy = pltpu.make_async_remote_copy(
            src_ref=fac.at[other],
            dst_ref=rfac.at[z],
            send_sem=fac_s.at[i],
            recv_sem=fac_r.at[i],
            device_id=in_line(other),
            device_id_type=MESH,
        )
        copy.start()
        fac_copies.append(copy)
    there_a = there(0, send_a, recv_a)
    rfac[z] = fac[z]
    recv_a[z] = send_a[z]

    for g in range(groups):
        for i in range(GROUP):
            h = g * GROUP + i
            gap = log_col[:, h : h + 1] - log_row[h : h + 1, :]
            cm[g, :, i * rows : (i + 1) * rows] = scale * jnp.exp(jnp.where(same, gap, -1e30))
        scores = contract(q_ref[:, lanes(g)], stack(k_ref[:, lanes(g)]), 1, 1)
        p = (scores * cm[g]).astype(BF16)
        probs[g] = p
        att[:, lanes(g)] = contract(p, stack(v_ref[:, lanes(g)]), 1, 0)

    def owner(phase, sign, there_copies, src, total, rtotal, rlfac, dst, come):
        order = list(range(RING)) if sign > 0 else list(reversed(range(RING)))
        line_copies = []
        back_copies = []

        def arrive(j):
            part = slice(j * step, (j + 1) * step)
            if phase == 0 and j == 0:
                for copy in fac_copies:
                    copy.wait_recv()
                product = rfac[0]
                for i in range(1, RING):
                    product = product * rfac[i]
                lfac[0] = product
            for copy in there_copies[j]:
                copy.wait_recv()
            run = src[order[0], part, :]
            for i in order[1:]:
                run = src[i, part, :] + rfac[i] * run
            total[part, :] = run
            these = []
            for k in range(1, REACH + 1):
                if j == 0:
                    copy = pltpu.make_async_remote_copy(
                        src_ref=lfac.at[0],
                        dst_ref=rlfac.at[k - 1],
                        send_sem=lfac_s.at[phase, k - 1],
                        recv_sem=lfac_r.at[phase, k - 1],
                        device_id=other_line(sign * k),
                        device_id_type=MESH,
                    )
                    copy.start()
                    these.append(copy)
                copy = pltpu.make_async_remote_copy(
                    src_ref=total.at[pl.ds(j * step, step)],
                    dst_ref=rtotal.at[k - 1, pl.ds(j * step, step)],
                    send_sem=line_s.at[phase, j, k - 1],
                    recv_sem=line_r.at[phase, j, k - 1],
                    device_id=other_line(sign * k),
                    device_id_type=MESH,
                )
                copy.start()
                these.append(copy)
            line_copies.append(these)

        def send_back(j):
            part = slice(j * step, (j + 1) * step)
            for copy in line_copies[j]:
                copy.wait_recv()
            run = rtotal[REACH - 1, part, :]
            for k in reversed(range(REACH - 1)):
                run = rtotal[k, part, :] + rlfac[k] * run
            for i in order:
                dst[i, part, :] = run
                run = src[i, part, :] + rfac[i] * run
            for i, k in enumerate(OFFSETS):
                other = ring(k)
                copy = pltpu.make_async_remote_copy(
                    src_ref=dst.at[other, pl.ds(j * step, step)],
                    dst_ref=come.at[z, pl.ds(j * step, step)],
                    send_sem=back_s.at[phase, j, i],
                    recv_sem=back_r.at[phase, j, i],
                    device_id=in_line(other),
                    device_id_type=MESH,
                )
                copy.start()
                back_copies.append(copy)

        for tick in range(PIECES + LAG):
            if tick < PIECES:
                arrive(tick)
            if tick >= LAG:
                send_back(tick - LAG)
        come[z] = dst[z]
        for copy in back_copies:
            copy.wait_recv()
        sent = [copy for these in there_copies + line_copies for copy in these] + back_copies
        return sent + (fac_copies if phase == 0 else [])

    sent = owner(0, 1, there_a, recv_a, tot_a, rtot_a, rlfac_a, back_a, come_a)

    square = jnp.zeros((rows, width), F32)
    inner = jnp.zeros((rows, width), F32)
    for g in range(groups):
        full = att[:, lanes(g)] + crx[:, lanes(g)] * contract(
            q_ref[:, lanes(g)], block_diagonal(come_a, g), 1, 0
        )
        att[:, lanes(g)] = full
        square += full * full
        inner += og_ref[:, lanes(g)].astype(F32) * gain(g) * full
    square = jnp.sum(square, axis=1, keepdims=True)
    inner = jnp.sum(inner, axis=1, keepdims=True)
    first = lax.broadcasted_iota(jnp.int32, (1, 128), 1) < 64
    sums[...] = jnp.where(first, square, inner)
    copy = pltpu.make_async_remote_copy(
        src_ref=sums,
        dst_ref=rsums,
        send_sem=sum_s,
        recv_sem=sum_r,
        device_id=(place, 1 - core),
        device_id_type=MESH,
    )
    copy.start()
    copy.wait()
    both = sums[...] + rsums[...]
    inv_rms = lax.rsqrt(both[:, 0:1] / feature_count + EPSILON)
    along = inv_rms * inv_rms * inv_rms * both[:, 64:65] / feature_count

    for g in range(groups):
        a = att[:, lanes(g)]
        gg = og_ref[:, lanes(g)].astype(F32) * gain(g)
        gr = (gg * inv_rms - a * along).astype(BF16)
        grad[:, lanes(g)] = gr
        reached = (q_ref[:, lanes(g)].astype(F32) * crx[:, lanes(g)]).astype(BF16)
        put_state(send_b, g, pick(contract(reached, gr, 0, 0)))
    there_b = there(1, send_b, recv_b)
    recv_b[z] = send_b[z]

    for g in range(groups):
        gr = grad[:, lanes(g)]
        o_ref[:, lanes(g)] = (att[:, lanes(g)] * inv_rms * gain(g)).astype(BF16)
        grad_scores = contract(gr, stack(v_ref[:, lanes(g)]), 1, 1)
        sg = (grad_scores * cm[g]).astype(BF16)
        dq = contract(sg, stack(k_ref[:, lanes(g)]), 1, 0) + crx[:, lanes(g)] * contract(
            gr, block_diagonal(come_a, g), 1, 1
        )
        dq_ref[:, lanes(g)] = dq.astype(BF16)
        p = probs[g]
        tall_p = jnp.concatenate([p[:, i * rows : (i + 1) * rows] for i in range(GROUP)], axis=0)
        tall_s = jnp.concatenate([sg[:, i * rows : (i + 1) * rows] for i in range(GROUP)], axis=0)
        kpart[:, lanes(g)] = contract(tall_s, stack(q_ref[:, lanes(g)]), 0, 0)
        vpart[:, lanes(g)] = contract(tall_p, stack(gr), 0, 0)

    sent += owner(1, -1, there_b, recv_b, tot_b, rtot_b, rlfac_b, back_b, come_b)

    for g in range(groups):
        later = block_diagonal(come_b, g)
        ex = xw[:, lanes(g)]
        dk_ref[:, lanes(g)] = (
            kpart[:, lanes(g)] + ex * contract(v_ref[:, lanes(g)], later, 1, 1)
        ).astype(BF16)
        dv_ref[:, lanes(g)] = (
            vpart[:, lanes(g)] + ex * contract(k_ref[:, lanes(g)], later, 1, 0)
        ).astype(BF16)
    for copy in sent:
        copy.wait_send()


def deliver(*refs):
    n = len(refs) // 2
    sems = refs[-1]
    copies = [pltpu.make_async_copy(refs[i], refs[n + i], sems.at[i]) for i in range(n)]
    for copy in copies:
        copy.start()
    for copy in copies:
        copy.wait()


def solution(mesh):
    lines = mesh.shape["ctx"] // RING
    cores = mesh.shape["head"]

    def on_device(queries, keys, values, decay_log, norm_gain, out_grad, doc_lengths):
        rows, local = queries.shape
        head_dim = local // decay_log.shape[0]
        width = GROUP * head_dim
        groups = local // width
        half = head_dim // 2
        assert groups * 2 == RING and half % (8 * PIECES) == 0
        vmem = pl.BlockSpec(memory_space=pltpu.VMEM)
        state = pltpu.VMEM((RING, half, width), F32)
        total = pltpu.VMEM((half, width), F32)
        totals = pltpu.VMEM((REACH, half, width), F32)
        wide = pltpu.VMEM((rows, local), F32)
        dma = pltpu.SemaphoreType.DMA
        n = len(OFFSETS)
        out = pltpu.VMEM((rows, local), BF16)
        results = pl.pallas_call(
            functools.partial(kernel, head_dim, local * cores, lines),
            out_shape=(out, out, out, out),
            in_specs=[pl.BlockSpec(memory_space=pltpu.SMEM)] + [vmem] * 6,
            out_specs=(vmem,) * 4,
            scratch_shapes=[
                wide,
                pltpu.VMEM((rows, local), BF16),
                wide,
                wide,
                pltpu.VMEM((groups, rows, GROUP * rows), F32),
                pltpu.VMEM((groups, rows, GROUP * rows), BF16),
                wide,
                wide,
                state, state, state, state,
                state, state, state, state,
                total, totals, total, totals,
                pltpu.VMEM((RING, 1, width), F32),
                pltpu.VMEM((RING, 1, width), F32),
                pltpu.VMEM((1, 1, width), F32),
                pltpu.VMEM((REACH, 1, width), F32),
                pltpu.VMEM((REACH, 1, width), F32),
                pltpu.VMEM((rows, 128), F32),
                pltpu.VMEM((rows, 128), F32),
                dma((2, PIECES, n)), dma((2, PIECES, n)),
                dma((2, PIECES, REACH)), dma((2, PIECES, REACH)),
                dma((2, PIECES, n)), dma((2, PIECES, n)),
                dma((n,)), dma((n,)),
                dma((2, REACH)), dma((2, REACH)),
                dma, dma,
            ],
            compiler_params=pltpu.CompilerParams(collective_id=0, has_side_effects=True),
        )(
            doc_lengths,
            queries,
            keys,
            values,
            decay_log,
            norm_gain.reshape(local // 128, 128),
            out_grad,
        )
        return pl.pallas_call(
            deliver,
            out_shape=(jax.ShapeDtypeStruct((rows, local), BF16),) * 4,
            in_specs=[vmem] * 4,
            out_specs=(pl.BlockSpec(memory_space=pl.ANY),) * 4,
            scratch_shapes=[dma((4,))],
        )(*[pltpu.with_memory_space_constraint(r, pltpu.VMEM) for r in results])

    return jax.shard_map(
        on_device,
        mesh=mesh,
        in_specs=(
            P("ctx", "head"),
            P("ctx", "head"),
            P("ctx", "head"),
            P("head", "ctx"),
            P("head"),
            P("ctx", "head"),
            P(),
        ),
        out_specs=(P("ctx", "head"),) * 4,
        check_vma=False,
    )
```

```python
import functools
import math

import jax
import jax.numpy as jnp
from jax import lax
from jax.experimental import pallas as pl
from jax.experimental.pallas import tpu as pltpu
from jax.sharding import PartitionSpec as P

EPSILON = 1e-06
MESH = pl.DeviceIdType.MESH
F32 = jnp.float32
BF16 = jnp.bfloat16

RING = 8
REACH = 4
GROUP = 4
OFFSETS = (4, 3, -3, 2, -2, 1, -1)
PIECES = 3
LAG = 1


def contract(a, b, ca, cb):
    return lax.dot_general(a, b, (((ca,), (cb,)), ((), ())), preferred_element_type=F32)


def kernel(
    head_dim,
    feature_count,
    lines,
    docs,
    q_ref,
    k_ref,
    v_ref,
    decay_ref,
    gain_ref,
    og_ref,
    o_ref,
    dq_ref,
    dk_ref,
    dv_ref,
    att,
    grad,
    crx,
    xw,
    cm,
    probs,
    kpart,
    vpart,
    send_a,
    recv_a,
    back_a,
    come_a,
    send_b,
    recv_b,
    back_b,
    come_b,
    tot_a,
    rtot_a,
    tot_b,
    rtot_b,
    fac,
    rfac,
    lfac,
    rlfac_a,
    rlfac_b,
    sums,
    rsums,
    there_s,
    there_r,
    line_s,
    line_r,
    back_s,
    back_r,
    fac_s,
    fac_r,
    lfac_s,
    lfac_r,
    sum_s,
    sum_r,
):
    rows = q_ref.shape[0]
    width = GROUP * head_dim
    groups = q_ref.shape[1] // width
    half = head_dim // 2
    scale = 1.0 / math.sqrt(head_dim)
    place = lax.axis_index("ctx")
    core = lax.axis_index("head")
    z = lax.rem(place, RING)
    line = lax.div(place, RING)

    def in_line(other):
        return (line * RING + other, core)

    def ring(offset):
        return lax.rem(z + (offset + RING), RING)

    def other_line(offset):
        return (lax.rem(line + (offset + lines), lines) * RING + z, core)

    barrier = pltpu.get_barrier_semaphore()
    partners = [in_line(ring(k)) for k in OFFSETS]
    partners += [other_line(s * k) for k in range(1, REACH + 1) for s in (1, -1)]
    partners += [(place, 1 - core)]
    for device in partners:
        pl.semaphore_signal(barrier, inc=1, device_id=device, device_id_type=MESH)

    start = place * rows
    col = start + lax.broadcasted_iota(jnp.int32, (rows, 1), 0)
    row = start + lax.broadcasted_iota(jnp.int32, (1, rows), 1)
    doc_col = jnp.zeros((rows, 1), jnp.int32)
    doc_row = jnp.zeros((1, rows), jnp.int32)
    before = jnp.int32(0)
    last = jnp.int32(0)
    begins = jnp.int32(0)
    for i in range(docs.shape[0]):
        doc_col += (begins <= col).astype(jnp.int32)
        doc_row += (begins <= row).astype(jnp.int32)
        before += (begins <= start - 1).astype(jnp.int32)
        last += (begins <= start + (rows - 1)).astype(jnp.int32)
        begins = begins + docs[i]
    carried_in = (doc_col == before).astype(F32)
    keep_last = (doc_col == last).astype(F32)
    same = jnp.logical_and(col >= row, doc_col == doc_row)

    decay = decay_ref[...]
    ti = lax.broadcasted_iota(jnp.int32, (rows, rows), 0)
    si = lax.broadcasted_iota(jnp.int32, (rows, rows), 1)
    lower = (si <= ti).astype(F32)
    log_col = lax.dot_general(
        lower, decay, (((1,), (1,)), ((), ())),
        precision=lax.Precision.HIGHEST, preferred_element_type=F32,
    )
    log_row = lax.dot_general(
        decay, lower, (((1,), (1,)), ((), ())),
        precision=lax.Precision.HIGHEST, preferred_element_type=F32,
    )
    exit_col = jnp.exp(log_col[rows - 1 : rows, :] - log_col) * keep_last
    reach_col = carried_in * jnp.exp(log_col)

    lane = lax.broadcasted_iota(jnp.int32, (1, width), 1)
    is_head = [
        jnp.logical_and(lane >= i * head_dim, lane < (i + 1) * head_dim) for i in range(GROUP)
    ]
    head_one = [m.astype(F32).astype(BF16) for m in is_head]

    def spread(columns, g):
        out = columns[:, g * GROUP + GROUP - 1 : g * GROUP + GROUP]
        for i in reversed(range(GROUP - 1)):
            out = jnp.where(is_head[i], columns[:, g * GROUP + i : g * GROUP + i + 1], out)
        return out

    def lanes(g):
        return slice(g * width, (g + 1) * width)

    def gain(g):
        tiles = width // 128
        return jnp.concatenate(
            [gain_ref[i : i + 1, :] for i in range(g * tiles, (g + 1) * tiles)], axis=1
        )

    def pick(square):
        out = square[(GROUP - 1) * head_dim :, :]
        for i in reversed(range(GROUP - 1)):
            out = jnp.where(is_head[i], square[i * head_dim : (i + 1) * head_dim, :], out)
        return out

    def stack(x):
        return jnp.concatenate([x * m for m in head_one], axis=0)

    def put_state(buf, g, state):
        buf[2 * g] = state[:half, :]
        buf[2 * g + 1] = state[half:, :]

    def block_diagonal(buf, g):
        state = jnp.concatenate([buf[2 * g], buf[2 * g + 1]], axis=0)
        return stack(state.astype(BF16))

    for g in range(groups):
        ex = spread(exit_col, g)
        xw[:, lanes(g)] = ex
        rx = spread(reach_col, g)
        crx[:, lanes(g)] = rx * scale
        fac[2 * g] = rx[rows - 1 : rows, :]
        fac[2 * g + 1] = rx[rows - 1 : rows, :]
        weighted = (k_ref[:, lanes(g)].astype(F32) * ex).astype(BF16)
        put_state(send_a, g, pick(contract(weighted, v_ref[:, lanes(g)], 0, 0)))

    pl.semaphore_wait(barrier, len(partners))

    step = half // PIECES

    def there(phase, src, dst):
        copies = []
        for j in range(PIECES):
            part = pl.ds(j * step, step)
            these = []
            for i, k in enumerate(OFFSETS):
                other = ring(k)
                copy = pltpu.make_async_remote_copy(
                    src_ref=src.at[other, part],
                    dst_ref=dst.at[z, part],
                    send_sem=there_s.at[phase, j, i],
                    recv_sem=there_r.at[phase, j, i],
                    device_id=in_line(other),
                    device_id_type=MESH,
                )
                copy.start()
                these.append(copy)
            copies.append(these)
        return copies

    fac_copies = []
    for i, k in enumerate(OFFSETS):
        other = ring(k)
        copy = pltpu.make_async_remote_copy(
            src_ref=fac.at[other],
            dst_ref=rfac.at[z],
            send_sem=fac_s.at[i],
            recv_sem=fac_r.at[i],
            device_id=in_line(other),
            device_id_type=MESH,
        )
        copy.start()
        fac_copies.append(copy)
    there_a = there(0, send_a, recv_a)
    rfac[z] = fac[z]
    recv_a[z] = send_a[z]

    for g in range(groups):
        for i in range(GROUP):
            h = g * GROUP + i
            gap = log_col[:, h : h + 1] - log_row[h : h + 1, :]
            cm[g, :, i * rows : (i + 1) * rows] = scale * jnp.exp(jnp.where(same, gap, -1e30))
        scores = contract(q_ref[:, lanes(g)], stack(k_ref[:, lanes(g)]), 1, 1)
        p = (scores * cm[g]).astype(BF16)
        probs[g] = p
        att[:, lanes(g)] = contract(p, stack(v_ref[:, lanes(g)]), 1, 0)

    def owner(phase, sign, there_copies, src, total, rtotal, rlfac, dst, come):
        order = list(range(RING)) if sign > 0 else list(reversed(range(RING)))
        line_copies = []
        back_copies = []

        def arrive(j):
            part = slice(j * step, (j + 1) * step)
            if phase == 0 and j == 0:
                for copy in fac_copies:
                    copy.wait_recv()
                product = rfac[0]
                for i in range(1, RING):
                    product = product * rfac[i]
                lfac[0] = product
            for copy in there_copies[j]:
                copy.wait_recv()
            run = src[order[0], part, :]
            for i in order[1:]:
                run = src[i, part, :] + rfac[i] * run
            total[part, :] = run
            these = []
            for k in range(1, REACH + 1):
                if j == 0:
                    copy = pltpu.make_async_remote_copy(
                        src_ref=lfac.at[0],
                        dst_ref=rlfac.at[k - 1],
                        send_sem=lfac_s.at[phase, k - 1],
                        recv_sem=lfac_r.at[phase, k - 1],
                        device_id=other_line(sign * k),
                        device_id_type=MESH,
                    )
                    copy.start()
                    these.append(copy)
                copy = pltpu.make_async_remote_copy(
                    src_ref=total.at[pl.ds(j * step, step)],
                    dst_ref=rtotal.at[k - 1, pl.ds(j * step, step)],
                    send_sem=line_s.at[phase, j, k - 1],
                    recv_sem=line_r.at[phase, j, k - 1],
                    device_id=other_line(sign * k),
                    device_id_type=MESH,
                )
                copy.start()
                these.append(copy)
            line_copies.append(these)

        def send_back(j):
            part = slice(j * step, (j + 1) * step)
            for copy in line_copies[j]:
                copy.wait_recv()
            run = rtotal[REACH - 1, part, :]
            for k in reversed(range(REACH - 1)):
                run = rtotal[k, part, :] + rlfac[k] * run
            for i in order:
                dst[i, part, :] = run
                run = src[i, part, :] + rfac[i] * run
            for i, k in enumerate(OFFSETS):
                other = ring(k)
                copy = pltpu.make_async_remote_copy(
                    src_ref=dst.at[other, pl.ds(j * step, step)],
                    dst_ref=come.at[z, pl.ds(j * step, step)],
                    send_sem=back_s.at[phase, j, i],
                    recv_sem=back_r.at[phase, j, i],
                    device_id=in_line(other),
                    device_id_type=MESH,
                )
                copy.start()
                back_copies.append(copy)

        for tick in range(PIECES + LAG):
            if tick < PIECES:
                arrive(tick)
            if tick >= LAG:
                send_back(tick - LAG)
        come[z] = dst[z]
        for copy in back_copies:
            copy.wait_recv()
        sent = [copy for these in there_copies + line_copies for copy in these] + back_copies
        return sent + (fac_copies if phase == 0 else [])

    sent = owner(0, 1, there_a, recv_a, tot_a, rtot_a, rlfac_a, back_a, come_a)

    square = jnp.zeros((rows, width), F32)
    inner = jnp.zeros((rows, width), F32)
    for g in range(groups):
        full = att[:, lanes(g)] + crx[:, lanes(g)] * contract(
            q_ref[:, lanes(g)], block_diagonal(come_a, g), 1, 0
        )
        att[:, lanes(g)] = full
        square += full * full
        inner += og_ref[:, lanes(g)].astype(F32) * gain(g) * full
    square = jnp.sum(square, axis=1, keepdims=True)
    inner = jnp.sum(inner, axis=1, keepdims=True)
    first = lax.broadcasted_iota(jnp.int32, (1, 128), 1) < 64
    sums[...] = jnp.where(first, square, inner)
    copy = pltpu.make_async_remote_copy(
        src_ref=sums,
        dst_ref=rsums,
        send_sem=sum_s,
        recv_sem=sum_r,
        device_id=(place, 1 - core),
        device_id_type=MESH,
    )
    copy.start()
    copy.wait()
    both = sums[...] + rsums[...]
    inv_rms = lax.rsqrt(both[:, 0:1] / feature_count + EPSILON)
    along = inv_rms * inv_rms * inv_rms * both[:, 64:65] / feature_count

    for g in range(groups):
        a = att[:, lanes(g)]
        gg = og_ref[:, lanes(g)].astype(F32) * gain(g)
        gr = (gg * inv_rms - a * along).astype(BF16)
        grad[:, lanes(g)] = gr
        reached = (q_ref[:, lanes(g)].astype(F32) * crx[:, lanes(g)]).astype(BF16)
        put_state(send_b, g, pick(contract(reached, gr, 0, 0)))
    there_b = there(1, send_b, recv_b)
    recv_b[z] = send_b[z]

    for g in range(groups):
        gr = grad[:, lanes(g)]
        o_ref[:, lanes(g)] = (att[:, lanes(g)] * inv_rms * gain(g)).astype(BF16)
        grad_scores = contract(gr, stack(v_ref[:, lanes(g)]), 1, 1)
        sg = (grad_scores * cm[g]).astype(BF16)
        dq = contract(sg, stack(k_ref[:, lanes(g)]), 1, 0) + crx[:, lanes(g)] * contract(
            gr, block_diagonal(come_a, g), 1, 1
        )
        dq_ref[:, lanes(g)] = dq.astype(BF16)
        p = probs[g]
        tall_p = jnp.concatenate([p[:, i * rows : (i + 1) * rows] for i in range(GROUP)], axis=0)
        tall_s = jnp.concatenate([sg[:, i * rows : (i + 1) * rows] for i in range(GROUP)], axis=0)
        kpart[:, lanes(g)] = contract(tall_s, stack(q_ref[:, lanes(g)]), 0, 0)
        vpart[:, lanes(g)] = contract(tall_p, stack(gr), 0, 0)

    sent += owner(1, -1, there_b, recv_b, tot_b, rtot_b, rlfac_b, back_b, come_b)

    for g in range(groups):
        later = block_diagonal(come_b, g)
        ex = xw[:, lanes(g)]
        dk_ref[:, lanes(g)] = (
            kpart[:, lanes(g)] + ex * contract(v_ref[:, lanes(g)], later, 1, 1)
        ).astype(BF16)
        dv_ref[:, lanes(g)] = (
            vpart[:, lanes(g)] + ex * contract(k_ref[:, lanes(g)], later, 1, 0)
        ).astype(BF16)
    for copy in sent:
        copy.wait_send()


def deliver(*refs):
    n = len(refs) // 2
    sems = refs[-1]
    copies = [pltpu.make_async_copy(refs[i], refs[n + i], sems.at[i]) for i in range(n)]
    for copy in copies:
        copy.start()
    for copy in copies:
        copy.wait()


def solution(mesh):
    lines = mesh.shape["ctx"] // RING
    cores = mesh.shape["head"]

    def on_device(queries, keys, values, decay_log, norm_gain, out_grad, doc_lengths):
        rows, local = queries.shape
        head_dim = local // decay_log.shape[0]
        width = GROUP * head_dim
        groups = local // width
        half = head_dim // 2
        assert groups * 2 == RING and half % (8 * PIECES) == 0
        vmem = pl.BlockSpec(memory_space=pltpu.VMEM)
        state = pltpu.VMEM((RING, half, width), F32)
        total = pltpu.VMEM((half, width), F32)
        totals = pltpu.VMEM((REACH, half, width), F32)
        wide = pltpu.VMEM((rows, local), F32)
        dma = pltpu.SemaphoreType.DMA
        n = len(OFFSETS)
        out = pltpu.VMEM((rows, local), BF16)
        results = pl.pallas_call(
            functools.partial(kernel, head_dim, local * cores, lines),
            out_shape=(out, out, out, out),
            in_specs=[pl.BlockSpec(memory_space=pltpu.SMEM)] + [vmem] * 6,
            out_specs=(vmem,) * 4,
            scratch_shapes=[
                wide,
                pltpu.VMEM((rows, local), BF16),
                wide,
                wide,
                pltpu.VMEM((groups, rows, GROUP * rows), F32),
                pltpu.VMEM((groups, rows, GROUP * rows), BF16),
                wide,
                wide,
                state, state, state, state,
                state, state, state, state,
                total, totals, total, totals,
                pltpu.VMEM((RING, 1, width), F32),
                pltpu.VMEM((RING, 1, width), F32),
                pltpu.VMEM((1, 1, width), F32),
                pltpu.VMEM((REACH, 1, width), F32),
                pltpu.VMEM((REACH, 1, width), F32),
                pltpu.VMEM((rows, 128), F32),
                pltpu.VMEM((rows, 128), F32),
                dma((2, PIECES, n)), dma((2, PIECES, n)),
                dma((2, PIECES, REACH)), dma((2, PIECES, REACH)),
                dma((2, PIECES, n)), dma((2, PIECES, n)),
                dma((n,)), dma((n,)),
                dma((2, REACH)), dma((2, REACH)),
                dma, dma,
            ],
            compiler_params=pltpu.CompilerParams(collective_id=0, has_side_effects=True),
        )(
            doc_lengths,
            queries,
            keys,
            values,
            decay_log,
            norm_gain.reshape(local // 128, 128),
            out_grad,
        )
        return pl.pallas_call(
            deliver,
            out_shape=(jax.ShapeDtypeStruct((rows, local), BF16),) * 4,
            in_specs=[vmem] * 4,
            out_specs=(pl.BlockSpec(memory_space=pl.ANY),) * 4,
            scratch_shapes=[dma((4,))],
        )(*[pltpu.with_memory_space_constraint(r, pltpu.VMEM) for r in results])

    return jax.shard_map(
        on_device,
        mesh=mesh,
        in_specs=(
            P("ctx", "head"),
            P("ctx", "head"),
            P("ctx", "head"),
            P("head", "ctx"),
            P("head"),
            P("ctx", "head"),
            P(),
        ),
        out_specs=(P("ctx", "head"),) * 4,
        check_vma=False,
    )
```

```python
import functools
import math

import jax
import jax.numpy as jnp
from jax import lax
from jax.experimental import pallas as pl
from jax.experimental.pallas import tpu as pltpu
from jax.sharding import PartitionSpec as P

EPSILON = 1e-06
MESH = pl.DeviceIdType.MESH
F32 = jnp.float32
BF16 = jnp.bfloat16

RING = 8
REACH = 4
GROUP = 4
LINE_ORDER = (2, 3, 1, 4)
OFFSETS = (4, 3, -3, 2, -2, 1, -1)
PIECES = 3
LAG = 1


def contract(a, b, ca, cb):
    return lax.dot_general(a, b, (((ca,), (cb,)), ((), ())), preferred_element_type=F32)


def kernel(
    head_dim,
    feature_count,
    lines,
    docs,
    q_ref,
    k_ref,
    v_ref,
    decay_ref,
    gain_ref,
    og_ref,
    o_ref,
    dq_ref,
    dk_ref,
    dv_ref,
    att,
    grad,
    crx,
    xw,
    cm,
    probs,
    kpart,
    vpart,
    send_a,
    recv_a,
    back_a,
    come_a,
    send_b,
    recv_b,
    back_b,
    come_b,
    tot_a,
    rtot_a,
    tot_b,
    rtot_b,
    fac,
    rfac,
    lfac,
    rlfac_a,
    rlfac_b,
    sums,
    rsums,
    there_s,
    there_r,
    line_s,
    line_r,
    back_s,
    back_r,
    fac_s,
    fac_r,
    lfac_s,
    lfac_r,
    sum_s,
    sum_r,
):
    rows = q_ref.shape[0]
    width = GROUP * head_dim
    groups = q_ref.shape[1] // width
    half = head_dim // 2
    scale = 1.0 / math.sqrt(head_dim)
    place = lax.axis_index("ctx")
    core = lax.axis_index("head")
    z = lax.rem(place, RING)
    line = lax.div(place, RING)

    def in_line(other):
        return (line * RING + other, core)

    def ring(offset):
        return lax.rem(z + (offset + RING), RING)

    def other_line(offset):
        return (lax.rem(line + (offset + lines), lines) * RING + z, core)

    barrier = pltpu.get_barrier_semaphore()
    partners = [in_line(ring(k)) for k in OFFSETS]
    partners += [other_line(s * k) for k in range(1, REACH + 1) for s in (1, -1)]
    partners += [(place, 1 - core)]
    for device in partners:
        pl.semaphore_signal(barrier, inc=1, device_id=device, device_id_type=MESH)

    start = place * rows
    col = start + lax.broadcasted_iota(jnp.int32, (rows, 1), 0)
    row = start + lax.broadcasted_iota(jnp.int32, (1, rows), 1)
    doc_col = jnp.zeros((rows, 1), jnp.int32)
    doc_row = jnp.zeros((1, rows), jnp.int32)
    before = jnp.int32(0)
    last = jnp.int32(0)
    begins = jnp.int32(0)
    for i in range(docs.shape[0]):
        doc_col += (begins <= col).astype(jnp.int32)
        doc_row += (begins <= row).astype(jnp.int32)
        before += (begins <= start - 1).astype(jnp.int32)
        last += (begins <= start + (rows - 1)).astype(jnp.int32)
        begins = begins + docs[i]
    carried_in = (doc_col == before).astype(F32)
    keep_last = (doc_col == last).astype(F32)
    same = jnp.logical_and(col >= row, doc_col == doc_row)

    decay = decay_ref[...]
    ti = lax.broadcasted_iota(jnp.int32, (rows, rows), 0)
    si = lax.broadcasted_iota(jnp.int32, (rows, rows), 1)
    lower = (si <= ti).astype(F32)
    log_col = lax.dot_general(
        lower, decay, (((1,), (1,)), ((), ())),
        precision=lax.Precision.HIGHEST, preferred_element_type=F32,
    )
    log_row = lax.dot_general(
        decay, lower, (((1,), (1,)), ((), ())),
        precision=lax.Precision.HIGHEST, preferred_element_type=F32,
    )
    exit_col = jnp.exp(log_col[rows - 1 : rows, :] - log_col) * keep_last
    reach_col = carried_in * jnp.exp(log_col)

    lane = lax.broadcasted_iota(jnp.int32, (1, width), 1)
    is_head = [
        jnp.logical_and(lane >= i * head_dim, lane < (i + 1) * head_dim) for i in range(GROUP)
    ]
    head_one = [m.astype(F32).astype(BF16) for m in is_head]

    def spread(columns, g):
        out = columns[:, g * GROUP + GROUP - 1 : g * GROUP + GROUP]
        for i in reversed(range(GROUP - 1)):
            out = jnp.where(is_head[i], columns[:, g * GROUP + i : g * GROUP + i + 1], out)
        return out

    def lanes(g):
        return slice(g * width, (g + 1) * width)

    def gain(g):
        tiles = width // 128
        return jnp.concatenate(
            [gain_ref[i : i + 1, :] for i in range(g * tiles, (g + 1) * tiles)], axis=1
        )

    def pick(square):
        out = square[(GROUP - 1) * head_dim :, :]
        for i in reversed(range(GROUP - 1)):
            out = jnp.where(is_head[i], square[i * head_dim : (i + 1) * head_dim, :], out)
        return out

    def stack(x):
        return jnp.concatenate([x * m for m in head_one], axis=0)

    def put_state(buf, g, state):
        buf[2 * g] = state[:half, :]
        buf[2 * g + 1] = state[half:, :]

    def block_diagonal(buf, g):
        state = jnp.concatenate([buf[2 * g], buf[2 * g + 1]], axis=0)
        return stack(state.astype(BF16))

    for g in range(groups):
        ex = spread(exit_col, g)
        xw[:, lanes(g)] = ex
        rx = spread(reach_col, g)
        crx[:, lanes(g)] = rx * scale
        fac[2 * g] = rx[rows - 1 : rows, :]
        fac[2 * g + 1] = rx[rows - 1 : rows, :]
        weighted = (k_ref[:, lanes(g)].astype(F32) * ex).astype(BF16)
        put_state(send_a, g, pick(contract(weighted, v_ref[:, lanes(g)], 0, 0)))

    pl.semaphore_wait(barrier, len(partners))

    step = half // PIECES

    def there(phase, src, dst):
        copies = []
        for j in range(PIECES):
            part = pl.ds(j * step, step)
            these = []
            for i, k in enumerate(OFFSETS):
                other = ring(k)
                copy = pltpu.make_async_remote_copy(
                    src_ref=src.at[other, part],
                    dst_ref=dst.at[z, part],
                    send_sem=there_s.at[phase, j, i],
                    recv_sem=there_r.at[phase, j, i],
                    device_id=in_line(other),
                    device_id_type=MESH,
                )
                copy.start()
                these.append(copy)
            copies.append(these)
        return copies

    fac_copies = []
    for i, k in enumerate(OFFSETS):
        other = ring(k)
        copy = pltpu.make_async_remote_copy(
            src_ref=fac.at[other],
            dst_ref=rfac.at[z],
            send_sem=fac_s.at[i],
            recv_sem=fac_r.at[i],
            device_id=in_line(other),
            device_id_type=MESH,
        )
        copy.start()
        fac_copies.append(copy)
    there_a = there(0, send_a, recv_a)
    rfac[z] = fac[z]
    recv_a[z] = send_a[z]

    for g in range(groups):
        for i in range(GROUP):
            h = g * GROUP + i
            gap = log_col[:, h : h + 1] - log_row[h : h + 1, :]
            cm[g, :, i * rows : (i + 1) * rows] = scale * jnp.exp(jnp.where(same, gap, -1e30))
        scores = contract(q_ref[:, lanes(g)], stack(k_ref[:, lanes(g)]), 1, 1)
        p = (scores * cm[g]).astype(BF16)
        probs[g] = p
        att[:, lanes(g)] = contract(p, stack(v_ref[:, lanes(g)]), 1, 0)

    def owner(phase, sign, there_copies, src, total, rtotal, rlfac, dst, come):
        order = list(range(RING)) if sign > 0 else list(reversed(range(RING)))
        line_copies = []
        back_copies = []

        def arrive(j):
            part = slice(j * step, (j + 1) * step)
            if phase == 0 and j == 0:
                for copy in fac_copies:
                    copy.wait_recv()
                product = rfac[0]
                for i in range(1, RING):
                    product = product * rfac[i]
                lfac[0] = product
            for copy in there_copies[j]:
                copy.wait_recv()
            run = src[order[0], part, :]
            for i in order[1:]:
                run = src[i, part, :] + rfac[i] * run
            total[part, :] = run
            these = []
            for k in LINE_ORDER:
                if j == 0:
                    copy = pltpu.make_async_remote_copy(
                        src_ref=lfac.at[0],
                        dst_ref=rlfac.at[k - 1],
                        send_sem=lfac_s.at[phase, k - 1],
                        recv_sem=lfac_r.at[phase, k - 1],
                        device_id=other_line(sign * k),
                        device_id_type=MESH,
                    )
                    copy.start()
                    these.append(copy)
                copy = pltpu.make_async_remote_copy(
                    src_ref=total.at[pl.ds(j * step, step)],
                    dst_ref=rtotal.at[k - 1, pl.ds(j * step, step)],
                    send_sem=line_s.at[phase, j, k - 1],
                    recv_sem=line_r.at[phase, j, k - 1],
                    device_id=other_line(sign * k),
                    device_id_type=MESH,
                )
                copy.start()
                these.append(copy)
            line_copies.append(these)

        def send_back(j):
            part = slice(j * step, (j + 1) * step)
            for copy in line_copies[j]:
                copy.wait_recv()
            run = rtotal[REACH - 1, part, :]
            for k in reversed(range(REACH - 1)):
                run = rtotal[k, part, :] + rlfac[k] * run
            for i in order:
                dst[i, part, :] = run
                run = src[i, part, :] + rfac[i] * run
            for i, k in enumerate(OFFSETS):
                other = ring(k)
                copy = pltpu.make_async_remote_copy(
                    src_ref=dst.at[other, pl.ds(j * step, step)],
                    dst_ref=come.at[z, pl.ds(j * step, step)],
                    send_sem=back_s.at[phase, j, i],
                    recv_sem=back_r.at[phase, j, i],
                    device_id=in_line(other),
                    device_id_type=MESH,
                )
                copy.start()
                back_copies.append(copy)

        for tick in range(PIECES + LAG):
            if tick < PIECES:
                arrive(tick)
            if tick >= LAG:
                send_back(tick - LAG)
        come[z] = dst[z]
        for copy in back_copies:
            copy.wait_recv()
        sent = [copy for these in there_copies + line_copies for copy in these] + back_copies
        return sent + (fac_copies if phase == 0 else [])

    sent = owner(0, 1, there_a, recv_a, tot_a, rtot_a, rlfac_a, back_a, come_a)

    square = jnp.zeros((rows, width), F32)
    inner = jnp.zeros((rows, width), F32)
    for g in range(groups):
        full = att[:, lanes(g)] + crx[:, lanes(g)] * contract(
            q_ref[:, lanes(g)], block_diagonal(come_a, g), 1, 0
        )
        att[:, lanes(g)] = full
        square += full * full
        inner += og_ref[:, lanes(g)].astype(F32) * gain(g) * full
    square = jnp.sum(square, axis=1, keepdims=True)
    inner = jnp.sum(inner, axis=1, keepdims=True)
    first = lax.broadcasted_iota(jnp.int32, (1, 128), 1) < 64
    sums[...] = jnp.where(first, square, inner)
    copy = pltpu.make_async_remote_copy(
        src_ref=sums,
        dst_ref=rsums,
        send_sem=sum_s,
        recv_sem=sum_r,
        device_id=(place, 1 - core),
        device_id_type=MESH,
    )
    copy.start()
    copy.wait()
    both = sums[...] + rsums[...]
    inv_rms = lax.rsqrt(both[:, 0:1] / feature_count + EPSILON)
    along = inv_rms * inv_rms * inv_rms * both[:, 64:65] / feature_count

    for g in range(groups):
        a = att[:, lanes(g)]
        gg = og_ref[:, lanes(g)].astype(F32) * gain(g)
        gr = (gg * inv_rms - a * along).astype(BF16)
        grad[:, lanes(g)] = gr
        reached = (q_ref[:, lanes(g)].astype(F32) * crx[:, lanes(g)]).astype(BF16)
        put_state(send_b, g, pick(contract(reached, gr, 0, 0)))
    there_b = there(1, send_b, recv_b)
    recv_b[z] = send_b[z]

    for g in range(groups):
        gr = grad[:, lanes(g)]
        o_ref[:, lanes(g)] = (att[:, lanes(g)] * inv_rms * gain(g)).astype(BF16)
        grad_scores = contract(gr, stack(v_ref[:, lanes(g)]), 1, 1)
        sg = (grad_scores * cm[g]).astype(BF16)
        dq = contract(sg, stack(k_ref[:, lanes(g)]), 1, 0) + crx[:, lanes(g)] * contract(
            gr, block_diagonal(come_a, g), 1, 1
        )
        dq_ref[:, lanes(g)] = dq.astype(BF16)
        p = probs[g]
        tall_p = jnp.concatenate([p[:, i * rows : (i + 1) * rows] for i in range(GROUP)], axis=0)
        tall_s = jnp.concatenate([sg[:, i * rows : (i + 1) * rows] for i in range(GROUP)], axis=0)
        kpart[:, lanes(g)] = contract(tall_s, stack(q_ref[:, lanes(g)]), 0, 0)
        vpart[:, lanes(g)] = contract(tall_p, stack(gr), 0, 0)

    sent += owner(1, -1, there_b, recv_b, tot_b, rtot_b, rlfac_b, back_b, come_b)

    for g in range(groups):
        later = block_diagonal(come_b, g)
        ex = xw[:, lanes(g)]
        dk_ref[:, lanes(g)] = (
            kpart[:, lanes(g)] + ex * contract(v_ref[:, lanes(g)], later, 1, 1)
        ).astype(BF16)
        dv_ref[:, lanes(g)] = (
            vpart[:, lanes(g)] + ex * contract(k_ref[:, lanes(g)], later, 1, 0)
        ).astype(BF16)
    for copy in sent:
        copy.wait_send()


def deliver(*refs):
    n = len(refs) // 2
    sems = refs[-1]
    copies = [pltpu.make_async_copy(refs[i], refs[n + i], sems.at[i]) for i in range(n)]
    for copy in copies:
        copy.start()
    for copy in copies:
        copy.wait()


def solution(mesh):
    lines = mesh.shape["ctx"] // RING
    cores = mesh.shape["head"]

    def on_device(queries, keys, values, decay_log, norm_gain, out_grad, doc_lengths):
        rows, local = queries.shape
        head_dim = local // decay_log.shape[0]
        width = GROUP * head_dim
        groups = local // width
        half = head_dim // 2
        assert groups * 2 == RING and half % (8 * PIECES) == 0
        vmem = pl.BlockSpec(memory_space=pltpu.VMEM)
        state = pltpu.VMEM((RING, half, width), F32)
        total = pltpu.VMEM((half, width), F32)
        totals = pltpu.VMEM((REACH, half, width), F32)
        wide = pltpu.VMEM((rows, local), F32)
        dma = pltpu.SemaphoreType.DMA
        n = len(OFFSETS)
        out = pltpu.VMEM((rows, local), BF16)
        results = pl.pallas_call(
            functools.partial(kernel, head_dim, local * cores, lines),
            out_shape=(out, out, out, out),
            in_specs=[pl.BlockSpec(memory_space=pltpu.SMEM)] + [vmem] * 6,
            out_specs=(vmem,) * 4,
            scratch_shapes=[
                wide,
                pltpu.VMEM((rows, local), BF16),
                wide,
                wide,
                pltpu.VMEM((groups, rows, GROUP * rows), F32),
                pltpu.VMEM((groups, rows, GROUP * rows), BF16),
                wide,
                wide,
                state, state, state, state,
                state, state, state, state,
                total, totals, total, totals,
                pltpu.VMEM((RING, 1, width), F32),
                pltpu.VMEM((RING, 1, width), F32),
                pltpu.VMEM((1, 1, width), F32),
                pltpu.VMEM((REACH, 1, width), F32),
                pltpu.VMEM((REACH, 1, width), F32),
                pltpu.VMEM((rows, 128), F32),
                pltpu.VMEM((rows, 128), F32),
                dma((2, PIECES, n)), dma((2, PIECES, n)),
                dma((2, PIECES, REACH)), dma((2, PIECES, REACH)),
                dma((2, PIECES, n)), dma((2, PIECES, n)),
                dma((n,)), dma((n,)),
                dma((2, REACH)), dma((2, REACH)),
                dma, dma,
            ],
            compiler_params=pltpu.CompilerParams(collective_id=0, has_side_effects=True),
        )(
            doc_lengths,
            queries,
            keys,
            values,
            decay_log,
            norm_gain.reshape(local // 128, 128),
            out_grad,
        )
        return pl.pallas_call(
            deliver,
            out_shape=(jax.ShapeDtypeStruct((rows, local), BF16),) * 4,
            in_specs=[vmem] * 4,
            out_specs=(pl.BlockSpec(memory_space=pl.ANY),) * 4,
            scratch_shapes=[dma((4,))],
        )(*[pltpu.with_memory_space_constraint(r, pltpu.VMEM) for r in results])

    return jax.shard_map(
        on_device,
        mesh=mesh,
        in_specs=(
            P("ctx", "head"),
            P("ctx", "head"),
            P("ctx", "head"),
            P("head", "ctx"),
            P("head"),
            P("ctx", "head"),
            P(),
        ),
        out_specs=(P("ctx", "head"),) * 4,
        check_vma=False,
    )
```
